32 devices in a mesh: groups: 2 (over x), chol: 16 (over z, y, core).
Axes of the slice: x: 2, y: 2, z: 4, core: 2. Of those that a mesh axis runs over, the one named last changes fastest.
Arguments:
- green: bfloat16 [8, 256, 1024], P('groups', 'chol'), parts along dimension 0, may hold values from -6 to 6
- chol_vecs: bfloat16 [192, 256, 1024], P('chol'), may hold values from -0.15625 to 0.15625, as said below
- cotangent: float32 [8], P('groups'), parts along dimension 0, may hold values from 1536 to 6144
Outputs:
- energy: float32 [8], P('groups'), parts along dimension 0
- grad_green: float32 [8, 256, 1024], P('groups', 'chol'), parts along dimension 0
The draws below stay inside these ranges and needn't reach their ends.
There are 2 independent parts, one for each index of `groups`. The reference program is written for one: setup_inputs(seed, part) draws one part's arguments, and reference() takes and returns one part's arrays. A program takes and returns all parts, laid end to end along the dimension named above; an argument that names none is the same for every part. Nothing has to cross between parts.
Inputs may be any that keep to these rules, and one draw needn't show every extreme that they name: `chol_vecs`: each vector's entries are of order 1024 ** -0.5 times a factor that changes slowly from vector to vector.
All inputs are finite; a program needn't handle non-finite values.
Results may differ from the reference program's by a relative error of at most 0.0029.
Values may be sent and summed in bfloat16 or wider, within the bound.
No kernel may reach another device: no remote copies, remote signals or barrier semaphores. Data moves between devices by JAX's collectives and lax.ppermute only.
A program may use at most 64 MiB of HBM per device.

```python
import math
import jax
import jax.numpy as jnp
from jax import lax

NBASIS = 1024
NOCC = 256
WALKERS = 4
NCHOL = 192


def draw_chol_vecs(key, part):
    position = jnp.arange(NCHOL, dtype=jnp.float32) / NCHOL
    values = jnp.clip(jax.random.normal(key, (NCHOL, NOCC, NBASIS), jnp.float32), -5.0, 5.0)
    decay = 3.0
    factors = decay ** (-0.5 * position)
    return (values * factors[:, None, None] * NBASIS ** (-0.5)).astype(jnp.bfloat16)


def level_of(stream_key, dims, split, smallest, largest):
    loudness, own = 1.0, jax.random.fold_in(stream_key, 6)
    for dim, shards_of in split:
        draws = jnp.exp(jax.random.uniform(jax.random.fold_in(own, dim), (shards_of,), jnp.float32, smallest / len(split), largest / len(split)))
        loudness = loudness * jnp.repeat(draws, dims[dim] // shards_of).reshape([-1 if axis == dim else 1 for axis in range(len(dims))])
    return loudness


def normal_values(rng, dims, spread, bound, shards=(), kind=jnp.bfloat16):
    result = jax.random.normal(rng, dims, jnp.float32) * spread
    if len(shards) > 0:
        result = level_of(rng, dims, shards, -0.22, 0.18) * result
    return jnp.clip(result, min=-bound, max=bound).astype(kind)


def setup_inputs(seed: int = 0, part: int = 0) -> dict:
    arg_keys = jax.random.split(jax.random.key(seed), 4)
    own_keys = jax.random.split(jax.random.fold_in(arg_keys[3], part), 4)
    return {
        "green": normal_values(own_keys[0], (WALKERS, NOCC, NBASIS), 1.0, 6.0, ((1, 16),)),
        "chol_vecs": draw_chol_vecs(jax.random.fold_in(arg_keys[3], 71), part),
        "cotangent": jnp.clip(jnp.exp(jax.random.uniform(own_keys[2], (WALKERS,), jnp.float32, math.log(1536.0), math.log(6144.0))), 1536.0, 6144.0),
    }


def reference(green, chol_vecs, cotangent):
    scale = 1.0 / (NOCC * NCHOL)
    per_block = 4 if NCHOL % 4 == 0 else 1
    blocks = chol_vecs.reshape(NCHOL // per_block, per_block, NOCC, NBASIS)
    green_wide = green.astype(jnp.float32)

    def step(carry, lblock):
        energy_acc, grad_acc = carry
        lwide = lblock.astype(jnp.float32)
        tmat = jnp.einsum('gip,wjp->wgij', lwide, green_wide)
        pairs = jnp.einsum('wgij,wgji->w', tmat, tmat)
        thalf = lax.optimization_barrier(tmat.astype(jnp.bfloat16)).astype(jnp.float32)
        gpart = jnp.einsum('wgki,gip->wkp', thalf, lwide)
        return (energy_acc + pairs, grad_acc + gpart), None

    start = (jnp.zeros((WALKERS,), jnp.float32), jnp.zeros((WALKERS, NOCC, NBASIS), jnp.float32))
    (energy_sum, grad_sum), unused = lax.scan(step, start, blocks)
    energy = -0.5 * scale * energy_sum
    grad_green = -scale * cotangent[:, None, None] * grad_sum
    return (energy, grad_green)
```

```python
import functools

import jax
import jax.numpy as jnp
from jax import lax
from jax.experimental import pallas as pl
from jax.experimental.pallas import tpu as pltpu
from jax.sharding import PartitionSpec as P


BLOCK = 4


def orders_of(bits):
    down = list(range(bits - 1, -1, -1))
    return (down, [0] + down[:-1])


def relative_chips(order):
    table = [0]
    for bit in order:
        table = table + [entry ^ (1 << bit) for entry in table]
    return table


def stage_pairs(orders, chips, stage):
    return [
        (2 * chip + core, 2 * (chip ^ (1 << orders[core][stage])) + core)
        for chip in range(chips)
        for core in range(2)
    ]


def grad_kernel(ids, gathered, own, other, send, keep, energy, vecs, rows, wide, total, sems):
    chips, walkers, part, basis = gathered.shape
    count, occupied = own.shape[:2]
    steps = count // BLOCK

    def copies(source, first):
        return [
            pltpu.make_async_copy(
                source.at[pl.ds(k * BLOCK, BLOCK)],
                vecs.at[pl.ds((first + k) * BLOCK, BLOCK)],
                sems.at[first + k],
            )
            for k in range(steps)
        ]

    pending = copies(own, 0) + copies(other, steps)
    for copy in pending:
        copy.start()

    target = rows if wide is None else wide
    for pos in range(chips):
        for w in range(walkers):
            at = pl.multiple_of(w * occupied + ids[pos] * part, part)
            target[pl.ds(at, part), :] = gathered[pos, w].astype(target.dtype)
    if wide is not None:
        rows[...] = wide[...].astype(rows.dtype)

    total[...] = jnp.zeros_like(total)

    def step(b, carry):
        pltpu.make_async_copy(
            own.at[pl.ds(0, BLOCK)], vecs.at[pl.ds(b * BLOCK, BLOCK)], sems.at[b]
        ).wait()
        block = vecs[pl.ds(b * BLOCK, BLOCK)]
        tall = []
        for w in range(walkers):
            mine = rows[w * occupied : (w + 1) * occupied, :]
            tall.append(
                jnp.concatenate(
                    [
                        lax.dot_general(
                            block[g], mine, (((1,), (1,)), ((), ())),
                            preferred_element_type=jnp.float32,
                        ).astype(jnp.bfloat16)
                        for g in range(BLOCK)
                    ],
                    axis=1,
                )
            )
        thalf = jnp.concatenate(tall, axis=0)
        total[...] += jnp.dot(
            thalf, block.reshape(BLOCK * occupied, basis), preferred_element_type=jnp.float32
        )
        return carry

    lax.fori_loop(0, 2 * steps, step, 0)

    for w in range(walkers):
        span = slice(w * occupied, (w + 1) * occupied)
        product = total[span, :] * rows[span, :].astype(jnp.float32)
        energy[w] = jnp.full(energy.shape[1:], jnp.sum(product), jnp.float32)
    half = chips // 2
    for pos in range(chips):
        for w in range(walkers):
            at = pl.multiple_of(w * occupied + ids[pos] * part, part)
            value = total[pl.ds(at, part), :]
            if pos < half:
                keep[pos, w] = value
            else:
                send[pos - half, w] = value.astype(jnp.bfloat16)


def partial_grads(ids, gathered, own, other):
    chips, walkers, part, basis = gathered.shape
    count, occupied = own.shape[:2]
    narrow = part % 16 == 0
    scratch = [
        pltpu.VMEM((2 * count, occupied, basis), jnp.bfloat16),
        pltpu.VMEM((walkers * occupied, basis), jnp.bfloat16),
    ]
    if not narrow:
        scratch.append(pltpu.VMEM((walkers * occupied, basis), jnp.float32))
    scratch += [
        pltpu.VMEM((walkers * occupied, basis), jnp.float32),
        pltpu.SemaphoreType.DMA((2 * count // BLOCK,)),
    ]

    def body(*refs):
        if narrow:
            refs = refs[:9] + (None,) + refs[9:]
        grad_kernel(*refs)

    half = chips // 2
    vmem = pl.BlockSpec(memory_space=pltpu.VMEM)
    anywhere = pl.BlockSpec(memory_space=pl.ANY)
    flops = 8 * walkers * count * occupied * occupied * basis
    return pl.pallas_call(
        body,
        out_shape=(
            jax.ShapeDtypeStruct((half, walkers, part, basis), jnp.bfloat16),
            jax.ShapeDtypeStruct((half, walkers, part, basis), jnp.float32),
            jax.ShapeDtypeStruct((walkers, 8, 128), jnp.float32),
        ),
        in_specs=[pl.BlockSpec(memory_space=pltpu.SMEM), vmem, anywhere, anywhere],
        out_specs=(vmem, vmem, vmem),
        scratch_shapes=scratch,
        compiler_params=pltpu.CompilerParams(vmem_limit_bytes=40 << 20),
        cost_estimate=pl.CostEstimate(
            flops=flops, bytes_accessed=4 * count * occupied * basis, transcendentals=0
        ),
        name="partial_grads",
    )(ids, gathered, own, other)


def per_device(green, chol_vecs, cotangent):
    size = lax.axis_size("chol")
    chips = size // 2
    bits = chips.bit_length() - 1
    orders = orders_of(bits)
    walkers, share, basis = green.shape
    pair = walkers // 2
    count, occupied = chol_vecs.shape[:2]
    scale = 1.0 / (occupied * count * size)
    index = lax.axis_index("chol")
    chip, core = index // 2, index % 2
    swap = [(d, d ^ 1) for d in range(size)]

    tables = [jnp.array(relative_chips(order), jnp.int32) for order in orders]
    ids = jnp.where(core == 0, tables[0], tables[1]) ^ chip

    theirs = lax.ppermute(green, "chol", swap)
    both = jnp.where(
        core == 0,
        jnp.concatenate([green, theirs], axis=1),
        jnp.concatenate([theirs, green], axis=1),
    )
    gathered = lax.dynamic_slice_in_dim(both, core * pair, pair, axis=0)[None]
    gathered, vecs = lax.optimization_barrier((gathered, chol_vecs))
    other = lax.ppermute(vecs, "chol", swap)

    for stage in range(bits):
        got = lax.ppermute(gathered, "chol", stage_pairs(orders, chips, stage))
        gathered = jnp.concatenate([gathered, got], axis=0)

    send, keep, energy = partial_grads(ids, gathered, chol_vecs, other)

    for stage in range(bits - 1, -1, -1):
        pairs = stage_pairs(orders, chips, stage)
        got = lax.ppermute(send, "chol", pairs)
        energy = energy + lax.ppermute(energy, "chol", pairs)
        keep = keep + got.astype(jnp.float32)
        if stage > 0:
            half = keep.shape[0] // 2
            keep, send = keep[:half], keep[half:].astype(jnp.bfloat16)

    rows = keep[0].reshape(pair, 2, share, basis)
    mine = lax.dynamic_index_in_dim(rows, core, axis=1, keepdims=False)
    away = lax.dynamic_index_in_dim(rows, 1 - core, axis=1, keepdims=False)
    back = lax.ppermute(away, "chol", swap)
    far_energy = lax.ppermute(energy, "chol", swap)
    grads = jnp.where(
        core == 0, jnp.concatenate([mine, back]), jnp.concatenate([back, mine])
    )
    sums = jnp.where(
        core == 0, jnp.concatenate([energy, far_energy]), jnp.concatenate([far_energy, energy])
    )[:, 0, 0]
    return (-0.5 * scale * sums, -scale * cotangent[:, None, None] * grads)


def solution(mesh):
    placed = (P("groups", "chol", None), P("chol", None, None), P("groups"))
    return jax.shard_map(
        per_device,
        mesh=mesh,
        in_specs=placed,
        out_specs=(P("groups"), P("groups", "chol", None)),
        check_vma=False,
    )
```

```python
import functools

import jax
import jax.numpy as jnp
from jax import lax
from jax.experimental import pallas as pl
from jax.experimental.pallas import tpu as pltpu
from jax.sharding import PartitionSpec as P


BLOCK = 4
BF16 = jnp.bfloat16
F32 = jnp.float32
VMEM = pl.BlockSpec(memory_space=pltpu.VMEM)
HBM = pl.BlockSpec(memory_space=pltpu.HBM)


def orders_of(bits):
    down = list(range(bits - 1, -1, -1))
    return (down, down[:-2] + down[:-3:-1])


def relative_chips(order):
    table = [0]
    for bit in order:
        table = table + [entry ^ (1 << bit) for entry in table]
    return table


def stage_pairs(orders, chips, stage):
    return [
        (2 * chip + core, 2 * (chip ^ (1 << orders[core][stage])) + core)
        for chip in range(chips)
        for core in range(2)
    ]


def walker_rows(gathered, w):
    chips, _, part, basis = gathered.shape
    return gathered[:, w].reshape(chips * part, basis)


def update(lhs, green_rows, rhs):
    vecs, m, basis = lhs.shape
    walkers = len(green_rows)
    i = green_rows[0].shape[0]
    tmat = lax.dot_general(
        lhs.reshape(vecs * m, basis),
        jnp.concatenate(green_rows, axis=0),
        (((1,), (1,)), ((), ())),
        preferred_element_type=F32,
    ).astype(BF16)
    thalf = jnp.concatenate(
        [
            jnp.concatenate(
                [tmat[g * m : (g + 1) * m, w * i : (w + 1) * i] for g in range(vecs)], axis=1
            )
            for w in range(walkers)
        ],
        axis=0,
    )
    return jnp.dot(thalf, rhs.reshape(vecs * i, basis), preferred_element_type=F32)


def arrange_kernel(tables, part, source, out, sems):
    index = lax.axis_index("chol")
    chip, core = index // 2, index % 2
    copies = []
    for k in range(source.shape[0] // BLOCK):
        for pos, (a, b) in enumerate(zip(*tables)):
            at = pl.multiple_of((chip ^ jnp.where(core == 0, a, b)) * part, part)
            copies.append(
                pltpu.make_async_copy(
                    source.at[pl.ds(k * BLOCK, BLOCK), pl.ds(at, part), :],
                    out.at[pl.ds(k * BLOCK, BLOCK), pl.ds(pos * part, part), :],
                    sems.at[k, pos],
                )
            )
    for copy in copies:
        copy.start()
    for copy in copies:
        copy.wait()


def first_kernel(gathered, own, other, total):
    half, walkers, part, basis = gathered.shape
    rows = [walker_rows(gathered, w) for w in range(walkers)]
    total[...] = jnp.zeros_like(total)
    for vecs in (own, other):

        def step(k, carry):
            block = vecs.at[pl.ds(k * BLOCK, BLOCK)]
            new = update(block[...], rows, block[:, : half * part, :])
            total[...] += new.reshape(total.shape)
            return carry

        lax.fori_loop(0, vecs.shape[0] // BLOCK, step, 0)


def second_kernel(own_half, gathered, target, own, other, total, out, energy, acc):
    half, walkers, part, basis = gathered.shape
    span = half * part
    first = own_half * span
    for w in range(walkers):
        acc[w * span : (w + 1) * span, :] = total[w, first : first + span, :]
    rows = [walker_rows(gathered, w) for w in range(walkers)]
    for vecs in (own, other):

        def step(k, carry):
            block = vecs.at[pl.ds(k * BLOCK, BLOCK)]
            acc[...] += update(
                block[:, first : first + span, :], rows, block[:, span : 2 * span, :]
            )
            return carry

        lax.fori_loop(0, vecs.shape[0] // BLOCK, step, 0)
    for w in range(walkers):
        value = acc[w * span : (w + 1) * span, :]
        product = value * walker_rows(target, w).astype(F32)
        energy[w] = jnp.full(energy.shape[1:], jnp.sum(product), F32)
        for pos in range(half):
            out[pos, w] = value[pos * part : (pos + 1) * part].astype(out.dtype)


def arrange(tables, part, vecs):
    return pl.pallas_call(
        functools.partial(arrange_kernel, tables, part),
        out_shape=jax.ShapeDtypeStruct(vecs.shape, vecs.dtype),
        in_specs=[HBM],
        out_specs=VMEM,
        scratch_shapes=[pltpu.SemaphoreType.DMA((vecs.shape[0] // BLOCK, len(tables[0])))],
        compiler_params=pltpu.CompilerParams(vmem_limit_bytes=8 << 20),
        cost_estimate=pl.CostEstimate(
            flops=0, bytes_accessed=4 * vecs.size, transcendentals=0
        ),
        name="arrange",
    )(vecs)


def first_half(gathered, own, other):
    half, walkers, part, basis = gathered.shape
    count, occupied = own.shape[:2]
    return pl.pallas_call(
        first_kernel,
        out_shape=jax.ShapeDtypeStruct((walkers, occupied, basis), F32),
        in_specs=[VMEM] * 3,
        out_specs=VMEM,
        compiler_params=pltpu.CompilerParams(vmem_limit_bytes=20 << 20),
        cost_estimate=pl.CostEstimate(
            flops=4 * walkers * count * occupied * occupied * basis,
            bytes_accessed=4 * count * occupied * basis,
            transcendentals=0,
        ),
        name="first_half",
    )(gathered, own, other)


def second_half(own_half, gathered, target, own, other, total, kind):
    half, walkers, part, basis = gathered.shape
    count, occupied = own.shape[:2]
    return pl.pallas_call(
        functools.partial(second_kernel, own_half),
        out_shape=(
            jax.ShapeDtypeStruct(gathered.shape, kind),
            jax.ShapeDtypeStruct((walkers, 8, 128), F32),
        ),
        in_specs=[VMEM] * 5,
        out_specs=(VMEM, VMEM),
        scratch_shapes=[pltpu.VMEM((walkers * half * part, basis), F32)],
        compiler_params=pltpu.CompilerParams(vmem_limit_bytes=20 << 20),
        cost_estimate=pl.CostEstimate(
            flops=2 * walkers * count * occupied * occupied * basis,
            bytes_accessed=2 * gathered.size,
            transcendentals=0,
        ),
        name="second_half",
    )(gathered, target, own, other, total)


def per_device(green, chol_vecs, cotangent):
    size = lax.axis_size("chol")
    chips = size // 2
    bits = chips.bit_length() - 1
    orders = orders_of(bits)
    tables = [relative_chips(order) for order in orders]
    walkers, share, basis = green.shape
    pair = walkers // 2
    count, occupied = chol_vecs.shape[:2]
    scale = 1.0 / (occupied * count * size)
    core = lax.axis_index("chol") % 2
    swap = [(d, d ^ 1) for d in range(size)]

    theirs = lax.ppermute(green, "chol", swap)
    both = jnp.where(
        core == 0,
        jnp.concatenate([green, theirs], axis=1),
        jnp.concatenate([theirs, green], axis=1),
    )
    gathered = lax.dynamic_slice_in_dim(both, core * pair, pair, axis=0)[None]
    gathered, vecs = lax.optimization_barrier((gathered, chol_vecs))
    other = lax.ppermute(vecs, "chol", swap)

    for stage in range(bits - 1):
        got = lax.ppermute(gathered, "chol", stage_pairs(orders, chips, stage))
        gathered = jnp.concatenate([gathered, got], axis=0)
    pairs = stage_pairs(orders, chips, bits - 1)
    got = lax.ppermute(gathered, "chol", pairs)
    own, other = (arrange(tables, 2 * share, part) for part in (chol_vecs, other))
    total = first_half(gathered, own, other)

    send, energy_away = second_half(1, got, got, own, other, total, BF16)
    arrived = lax.ppermute(send, "chol", pairs)
    keep, energy_here = second_half(0, got, gathered, own, other, total, F32)
    energy = energy_away + energy_here

    for stage in range(bits - 1, -1, -1):
        pairs = stage_pairs(orders, chips, stage)
        if stage < bits - 1:
            arrived = lax.ppermute(send, "chol", pairs)
        arrived, met = lax.optimization_barrier(
            (arrived, lax.ppermute(energy, "chol", pairs))
        )
        energy = energy + met
        keep = keep + arrived.astype(F32)
        if stage > 0:
            half = keep.shape[0] // 2
            keep, send = keep[:half], keep[half:].astype(BF16)

    rows = keep[0].reshape(pair, 2, share, basis)
    mine = lax.dynamic_index_in_dim(rows, core, axis=1, keepdims=False)
    away = lax.dynamic_index_in_dim(rows, 1 - core, axis=1, keepdims=False)
    back = lax.ppermute(away, "chol", swap)
    far_energy = lax.ppermute(energy, "chol", swap)
    grads = jnp.where(
        core == 0, jnp.concatenate([mine, back]), jnp.concatenate([back, mine])
    )
    sums = jnp.where(
        core == 0, jnp.concatenate([energy, far_energy]), jnp.concatenate([far_energy, energy])
    )[:, 0, 0]
    return (-0.5 * scale * sums, -scale * cotangent[:, None, None] * grads)


def solution(mesh):
    placed = (P("groups", "chol", None), P("chol", None, None), P("groups"))
    return jax.shard_map(
        per_device,
        mesh=mesh,
        in_specs=placed,
        out_specs=(P("groups"), P("groups", "chol", None)),
        check_vma=False,
    )
```

```python
import functools

import jax
import jax.numpy as jnp
from jax import lax
from jax.experimental import pallas as pl
from jax.experimental.pallas import tpu as pltpu
from jax.sharding import PartitionSpec as P


BLOCK = 8
COPIED = 4
ROWS = 256
BF16 = jnp.bfloat16
F32 = jnp.float32
VMEM = pl.BlockSpec(memory_space=pltpu.VMEM)
HBM = pl.BlockSpec(memory_space=pltpu.HBM)


def orders_of(bits):
    down = list(range(bits - 1, -1, -1))
    return (down, down[:-2] + down[:-3:-1])


def relative_chips(order):
    table = [0]
    for bit in order:
        table = table + [entry ^ (1 << bit) for entry in table]
    return table


def stage_pairs(orders, chips, stage):
    return [
        (2 * chip + core, 2 * (chip ^ (1 << orders[core][stage])) + core)
        for chip in range(chips)
        for core in range(2)
    ]


def walker_rows(gathered, w):
    chips, _, part, basis = gathered.shape
    return gathered[:, w].reshape(chips * part, basis)


def tmat_half(lhs, green):
    vecs, m, basis = lhs.shape
    pack = max(1, ROWS // m)
    return jnp.concatenate(
        [
            lax.dot_general(
                lhs[g : g + pack].reshape(pack * m, basis), green, (((1,), (1,)), ((), ())),
                preferred_element_type=F32,
            ).astype(BF16)
            for g in range(0, vecs, pack)
        ],
        axis=0,
    )


def side_by_side(tmat, walkers, vecs):
    m, i = tmat.shape[0] // vecs, tmat.shape[1] // walkers
    return jnp.concatenate(
        [
            jnp.concatenate(
                [tmat[g * m : (g + 1) * m, w * i : (w + 1) * i] for g in range(vecs)], axis=1
            )
            for w in range(walkers)
        ],
        axis=0,
    )


def sweep(vecs, green, walkers, lhs_rows, rhs_rows, held, add):
    def step(k, carry):
        block = pl.ds(k * BLOCK, BLOCK)
        tmat = tmat_half(vecs[block, lhs_rows[0] : lhs_rows[1], :], green)
        held[...] = side_by_side(tmat, walkers, BLOCK)
        rhs = vecs[block, rhs_rows[0] : rhs_rows[1], :].reshape(-1, vecs.shape[2])
        add(jnp.dot(held[...], rhs, preferred_element_type=F32))
        return carry

    lax.fori_loop(0, vecs.shape[0] // BLOCK, step, 0)


def arrange_kernel(tables, part, first, source, *refs):
    out, sems = refs[-2:]
    index = lax.axis_index("chol")
    chip, core = index // 2, index % 2
    copies = []
    for k in range(source.shape[0] // COPIED):
        for pos, (a, b) in enumerate(zip(*tables)):
            at = pl.multiple_of((chip ^ jnp.where(core == 0, a, b)) * part, part)
            copies.append(
                pltpu.make_async_copy(
                    source.at[pl.ds(k * COPIED, COPIED), pl.ds(at, part), :],
                    out.at[pl.ds(first + k * COPIED, COPIED), pl.ds(pos * part, part), :],
                    sems.at[k, pos],
                )
            )
    for copy in copies:
        copy.start()
    for copy in copies:
        copy.wait()


def first_kernel(gathered, vecs, total, held):
    half, walkers, part, basis = gathered.shape
    span = half * part
    green = jnp.concatenate([walker_rows(gathered, w) for w in range(walkers)], axis=0)
    total[...] = jnp.zeros_like(total)

    def add(new):
        total[...] += new.reshape(total.shape)

    sweep(vecs, green, walkers, (0, 2 * span), (0, span), held, add)


def second_kernel(own_half, gathered, target, vecs, total, out, energy, acc, held):
    half, walkers, part, basis = gathered.shape
    span = half * part
    first = own_half * span
    green = jnp.concatenate([walker_rows(gathered, w) for w in range(walkers)], axis=0)
    for w in range(walkers):
        acc[w * span : (w + 1) * span, :] = total[w, first : first + span, :]

    def add(new):
        acc[...] += new

    sweep(vecs, green, walkers, (first, first + span), (span, 2 * span), held, add)
    for w in range(walkers):
        value = acc[w * span : (w + 1) * span, :]
        product = value * walker_rows(target, w).astype(F32)
        energy[w] = jnp.full(energy.shape[1:], jnp.sum(product), F32)
        for pos in range(half):
            out[pos, w] = value[pos * part : (pos + 1) * part].astype(out.dtype)


def arrange(tables, part, source, vecs=None):
    count = source.shape[0]
    args = (source,) if vecs is None else (source, vecs)
    return pl.pallas_call(
        functools.partial(arrange_kernel, tables, part, 0 if vecs is None else count),
        out_shape=jax.ShapeDtypeStruct((2 * count,) + source.shape[1:], source.dtype),
        in_specs=[HBM, VMEM][: len(args)],
        out_specs=VMEM,
        input_output_aliases={} if vecs is None else {1: 0},
        scratch_shapes=[pltpu.SemaphoreType.DMA((count // COPIED, len(tables[0])))],
        compiler_params=pltpu.CompilerParams(vmem_limit_bytes=8 << 20),
        cost_estimate=pl.CostEstimate(
            flops=0, bytes_accessed=4 * source.size, transcendentals=0
        ),
        name="arrange",
    )(*args)


def first_half(gathered, vecs):
    half, walkers, part, basis = gathered.shape
    count, occupied = vecs.shape[:2]
    return pl.pallas_call(
        first_kernel,
        out_shape=jax.ShapeDtypeStruct((walkers, occupied, basis), F32),
        in_specs=[VMEM] * 2,
        out_specs=VMEM,
        scratch_shapes=[pltpu.VMEM((walkers * occupied, BLOCK * half * part), BF16)],
        compiler_params=pltpu.CompilerParams(vmem_limit_bytes=20 << 20),
        cost_estimate=pl.CostEstimate(
            flops=2 * walkers * count * occupied * occupied * basis,
            bytes_accessed=2 * count * occupied * basis,
            transcendentals=0,
        ),
        name="first_half",
    )(gathered, vecs)


def second_half(own_half, gathered, target, vecs, total, kind):
    half, walkers, part, basis = gathered.shape
    count, occupied = vecs.shape[:2]
    return pl.pallas_call(
        functools.partial(second_kernel, own_half),
        out_shape=(
            jax.ShapeDtypeStruct(gathered.shape, kind),
            jax.ShapeDtypeStruct((walkers, 8, 128), F32),
        ),
        in_specs=[VMEM] * 4,
        out_specs=(VMEM, VMEM),
        scratch_shapes=[
            pltpu.VMEM((walkers * half * part, basis), F32),
            pltpu.VMEM((walkers * half * part, BLOCK * half * part), BF16),
        ],
        compiler_params=pltpu.CompilerParams(vmem_limit_bytes=20 << 20),
        cost_estimate=pl.CostEstimate(
            flops=walkers * count * occupied * occupied * basis,
            bytes_accessed=2 * gathered.size,
            transcendentals=0,
        ),
        name="second_half",
    )(gathered, target, vecs, total)


def per_device(green, chol_vecs, cotangent):
    size = lax.axis_size("chol")
    chips = size // 2
    bits = chips.bit_length() - 1
    orders = orders_of(bits)
    tables = [relative_chips(order) for order in orders]
    walkers, share, basis = green.shape
    pair = walkers // 2
    count, occupied = chol_vecs.shape[:2]
    scale = 1.0 / (occupied * count * size)
    core = lax.axis_index("chol") % 2
    swap = [(d, d ^ 1) for d in range(size)]

    theirs = lax.ppermute(green, "chol", swap)
    both = jnp.where(
        core == 0,
        jnp.concatenate([green, theirs], axis=1),
        jnp.concatenate([theirs, green], axis=1),
    )
    gathered = lax.dynamic_slice_in_dim(both, core * pair, pair, axis=0)[None]
    gathered, vecs = lax.optimization_barrier((gathered, chol_vecs))
    other = lax.ppermute(vecs, "chol", swap)

    for stage in range(bits - 1):
        got = lax.ppermute(gathered, "chol", stage_pairs(orders, chips, stage))
        gathered = jnp.concatenate([gathered, got], axis=0)
    pairs = stage_pairs(orders, chips, bits - 1)
    got = lax.ppermute(gathered, "chol", pairs)
    vecs = arrange(tables, 2 * share, other, arrange(tables, 2 * share, chol_vecs))
    total = first_half(gathered, vecs)

    send, energy_away = second_half(1, got, got, vecs, total, BF16)
    arrived = lax.ppermute(send, "chol", pairs)
    keep, energy_here = second_half(0, got, gathered, vecs, total, F32)
    energy = energy_away + energy_here

    for stage in range(bits - 1, -1, -1):
        pairs = stage_pairs(orders, chips, stage)
        if stage < bits - 1:
            arrived = lax.ppermute(send, "chol", pairs)
        arrived, met = lax.optimization_barrier(
            (arrived, lax.ppermute(energy, "chol", pairs))
        )
        energy = energy + met
        keep = keep + arrived.astype(F32)
        if stage > 0:
            half = keep.shape[0] // 2
            keep, send = keep[:half], keep[half:].astype(BF16)

    rows = keep[0].reshape(pair, 2, share, basis)
    mine = lax.dynamic_index_in_dim(rows, core, axis=1, keepdims=False)
    away = lax.dynamic_index_in_dim(rows, 1 - core, axis=1, keepdims=False)
    back = lax.ppermute(away, "chol", swap)
    far_energy = lax.ppermute(energy, "chol", swap)
    grads = jnp.where(
        core == 0, jnp.concatenate([mine, back]), jnp.concatenate([back, mine])
    )
    sums = jnp.where(
        core == 0, jnp.concatenate([energy, far_energy]), jnp.concatenate([far_energy, energy])
    )[:, 0, 0]
    return (-0.5 * scale * sums, -scale * cotangent[:, None, None] * grads)


def solution(mesh):
    placed = (P("groups", "chol", None), P("chol", None, None), P("groups"))
    return jax.shard_map(
        per_device,
        mesh=mesh,
        in_specs=placed,
        out_specs=(P("groups"), P("groups", "chol", None)),
        check_vma=False,
    )
```

```python
import functools

import jax
import jax.numpy as jnp
from jax import lax
from jax.experimental import pallas as pl
from jax.experimental.pallas import tpu as pltpu
from jax.sharding import PartitionSpec as P


BLOCK = 8
COPIED = 4
ROWS = 256
BF16 = jnp.bfloat16
F32 = jnp.float32
VMEM = pl.BlockSpec(memory_space=pltpu.VMEM)
HBM = pl.BlockSpec(memory_space=pltpu.HBM)


def orders_of(bits):
    down = list(range(bits - 1, -1, -1))
    return (down, down[:-2] + down[:-3:-1])


def relative_chips(order):
    table = [0]
    for bit in order:
        table = table + [entry ^ (1 << bit) for entry in table]
    return table


def stage_pairs(orders, chips, stage):
    return [
        (2 * chip + core, 2 * (chip ^ (1 << orders[core][stage])) + core)
        for chip in range(chips)
        for core in range(2)
    ]


def walker_rows(gathered, w):
    chips, _, part, basis = gathered.shape
    return gathered[:, w].reshape(chips * part, basis)


def tmat_half(lhs, green):
    vecs, m, basis = lhs.shape
    pack = max(1, ROWS // m)
    return jnp.concatenate(
        [
            lax.dot_general(
                lhs[g : g + pack].reshape(pack * m, basis), green, (((1,), (1,)), ((), ())),
                preferred_element_type=F32,
            ).astype(BF16)
            for g in range(0, vecs, pack)
        ],
        axis=0,
    )


def side_by_side(tmat, walkers, vecs):
    m, i = tmat.shape[0] // vecs, tmat.shape[1] // walkers
    return jnp.concatenate(
        [
            jnp.concatenate(
                [tmat[g * m : (g + 1) * m, w * i : (w + 1) * i] for g in range(vecs)], axis=1
            )
            for w in range(walkers)
        ],
        axis=0,
    )


def sweep(vecs, green, walkers, lhs_rows, rhs_rows, held, add):
    def step(k, carry):
        block = pl.ds(k * BLOCK, BLOCK)
        tmat = tmat_half(vecs[block, lhs_rows[0] : lhs_rows[1], :], green)
        held[...] = side_by_side(tmat, walkers, BLOCK)
        rhs = vecs[block, rhs_rows[0] : rhs_rows[1], :].reshape(-1, vecs.shape[2])
        add(jnp.dot(held[...], rhs, preferred_element_type=F32))
        return carry

    lax.fori_loop(0, vecs.shape[0] // BLOCK, step, 0)


def arrange_kernel(tables, part, first, source, *refs):
    out, sems = refs[-2:]
    index = lax.axis_index("chol")
    chip, core = index // 2, index % 2
    copies = []
    for k in range(source.shape[0] // COPIED):
        for pos, (a, b) in enumerate(zip(*tables)):
            at = pl.multiple_of((chip ^ jnp.where(core == 0, a, b)) * part, part)
            copies.append(
                pltpu.make_async_copy(
                    source.at[pl.ds(k * COPIED, COPIED), pl.ds(at, part), :],
                    out.at[pl.ds(first + k * COPIED, COPIED), pl.ds(pos * part, part), :],
                    sems.at[k, pos],
                )
            )
    for copy in copies:
        copy.start()
    for copy in copies:
        copy.wait()


def first_kernel(gathered, vecs, total, held):
    half, walkers, part, _ = gathered.shape
    span = half * part
    green = jnp.concatenate([walker_rows(gathered, w) for w in range(walkers)], axis=0)
    total[...] = jnp.zeros_like(total)

    def add(new):
        total[...] += new.reshape(total.shape)

    sweep(vecs, green, walkers, (0, 2 * span), (0, span), held, add)


def second_kernel(own_half, gathered, target, vecs, total, out, energy, acc, held):
    half, walkers, part, _ = gathered.shape
    span = half * part
    first = own_half * span
    green = jnp.concatenate([walker_rows(gathered, w) for w in range(walkers)], axis=0)
    for w in range(walkers):
        acc[w * span : (w + 1) * span, :] = total[w, first : first + span, :]

    def add(new):
        acc[...] += new

    sweep(vecs, green, walkers, (first, first + span), (span, 2 * span), held, add)
    for w in range(walkers):
        value = acc[w * span : (w + 1) * span, :]
        product = value * walker_rows(target, w).astype(F32)
        energy[w] = jnp.full(energy.shape[1:], jnp.sum(product), F32)
        for pos in range(half):
            out[pos, w] = value[pos * part : (pos + 1) * part].astype(out.dtype)


def arrange(tables, part, source, vecs=None):
    count = source.shape[0]
    args = (source,) if vecs is None else (source, vecs)
    return pl.pallas_call(
        functools.partial(arrange_kernel, tables, part, 0 if vecs is None else count),
        out_shape=jax.ShapeDtypeStruct((2 * count,) + source.shape[1:], source.dtype),
        in_specs=[HBM, VMEM][: len(args)],
        out_specs=VMEM,
        input_output_aliases={} if vecs is None else {1: 0},
        scratch_shapes=[pltpu.SemaphoreType.DMA((count // COPIED, len(tables[0])))],
        compiler_params=pltpu.CompilerParams(vmem_limit_bytes=8 << 20),
        cost_estimate=pl.CostEstimate(
            flops=0, bytes_accessed=4 * source.size, transcendentals=0
        ),
        name="arrange",
    )(*args)


def first_half(gathered, vecs):
    half, walkers, part, basis = gathered.shape
    count, occupied = vecs.shape[:2]
    return pl.pallas_call(
        first_kernel,
        out_shape=jax.ShapeDtypeStruct((walkers, occupied, basis), F32),
        in_specs=[VMEM] * 2,
        out_specs=VMEM,
        scratch_shapes=[pltpu.VMEM((walkers * occupied, BLOCK * half * part), BF16)],
        compiler_params=pltpu.CompilerParams(vmem_limit_bytes=20 << 20),
        cost_estimate=pl.CostEstimate(
            flops=2 * walkers * count * occupied * occupied * basis,
            bytes_accessed=2 * count * occupied * basis,
            transcendentals=0,
        ),
        name="first_half",
    )(gathered, vecs)


def second_half(own_half, gathered, target, vecs, total, kind):
    half, walkers, part, basis = gathered.shape
    count, occupied = vecs.shape[:2]
    return pl.pallas_call(
        functools.partial(second_kernel, own_half),
        out_shape=(
            jax.ShapeDtypeStruct(gathered.shape, kind),
            jax.ShapeDtypeStruct((walkers, 8, 128), F32),
        ),
        in_specs=[VMEM] * 4,
        out_specs=(VMEM, VMEM),
        scratch_shapes=[
            pltpu.VMEM((walkers * half * part, basis), F32),
            pltpu.VMEM((walkers * half * part, BLOCK * half * part), BF16),
        ],
        compiler_params=pltpu.CompilerParams(vmem_limit_bytes=20 << 20),
        cost_estimate=pl.CostEstimate(
            flops=walkers * count * occupied * occupied * basis,
            bytes_accessed=2 * gathered.size,
            transcendentals=0,
        ),
        name="second_half",
    )(gathered, target, vecs, total)


def shift(x, pairs):
    return lax.ppermute(x, "chol", pairs)


def per_device(green, chol_vecs, cotangent):
    size = lax.axis_size("chol")
    chips = size // 2
    bits = chips.bit_length() - 1
    orders = orders_of(bits)
    tables = [relative_chips(order) for order in orders]
    walkers, share, basis = green.shape
    pair = walkers // 2
    count, occupied = chol_vecs.shape[:2]
    scale = 1.0 / (occupied * count * size)
    core = lax.axis_index("chol") % 2
    swap = [(d, d ^ 1) for d in range(size)]

    far = stage_pairs(orders, chips, 0)
    cross = [(source, target ^ 1) for source, target in far]

    def ordered(same, opposite, axis):
        return jnp.where(
            core == 0,
            jnp.concatenate([same, opposite], axis=axis),
            jnp.concatenate([opposite, same], axis=axis),
        )

    def split(x, axis):
        return (
            lax.dynamic_index_in_dim(x, core, axis=axis, keepdims=False),
            lax.dynamic_index_in_dim(x, 1 - core, axis=axis, keepdims=False),
        )

    mine, theirs = split(green.reshape(2, pair, share, basis), 0)
    far_same = shift(mine, far)
    far_cross = shift(theirs, cross)
    near_cross = shift(theirs, swap)
    near_cross, vecs = lax.optimization_barrier((near_cross, chol_vecs))
    other = shift(vecs, swap)
    gathered = jnp.stack(
        [ordered(mine, near_cross, 1), ordered(far_same, far_cross, 1)]
    )

    for stage in range(1, bits - 1):
        got = lax.ppermute(gathered, "chol", stage_pairs(orders, chips, stage))
        gathered = jnp.concatenate([gathered, got], axis=0)
    pairs = stage_pairs(orders, chips, bits - 1)
    got = lax.ppermute(gathered, "chol", pairs)
    vecs = arrange(tables, 2 * share, other, arrange(tables, 2 * share, chol_vecs))
    total = first_half(gathered, vecs)

    send, energy_away = second_half(1, got, got, vecs, total, BF16)
    arrived = lax.ppermute(send, "chol", pairs)
    keep, energy_here = second_half(0, got, gathered, vecs, total, F32)
    energy = energy_away + energy_here

    for stage in range(bits - 1, 0, -1):
        pairs = stage_pairs(orders, chips, stage)
        if stage < bits - 1:
            arrived = lax.ppermute(send, "chol", pairs)
        arrived, met = lax.optimization_barrier(
            (arrived, lax.ppermute(energy, "chol", pairs))
        )
        energy = energy + met
        keep = keep + arrived.astype(F32)
        if stage > 1:
            half = keep.shape[0] // 2
            keep, send = keep[:half], keep[half:].astype(BF16)

    (near_here, far_here), (near_there, far_there) = split(
        keep.reshape(2, pair, 2, share, basis), 2
    )
    here = shift(far_here.astype(BF16), far)
    there = shift(far_there.astype(BF16), cross)
    back = shift(near_there, swap)
    sums = ordered(
        energy + shift(energy, far), shift(energy, swap) + shift(energy, cross), 0
    )[:, 0, 0]
    grads = ordered(near_here + here.astype(F32), back + there.astype(F32), 0)
    return (-0.5 * scale * sums, -scale * cotangent[:, None, None] * grads)


def solution(mesh):
    placed = (P("groups", "chol", None), P("chol", None, None), P("groups"))
    return jax.shard_map(
        per_device,
        mesh=mesh,
        in_specs=placed,
        out_specs=(P("groups"), P("groups", "chol", None)),
        check_vma=False,
    )
```

```python
import functools

import jax
import jax.numpy as jnp
from jax import lax
from jax.experimental import pallas as pl
from jax.experimental.pallas import tpu as pltpu
from jax.sharding import PartitionSpec as P


BLOCK = 8
COPIED = 4
ROWS = 256
BF16 = jnp.bfloat16
F32 = jnp.float32
VMEM = pl.BlockSpec(memory_space=pltpu.VMEM)
HBM = pl.BlockSpec(memory_space=pltpu.HBM)


def orders_of(bits):
    down = list(range(bits - 1, -1, -1))
    return (down, down[:-2] + down[:-3:-1])


def relative_chips(order):
    table = [0]
    for bit in order:
        table = table + [entry ^ (1 << bit) for entry in table]
    return table


def stage_pairs(orders, chips, stage):
    return [
        (2 * chip + core, 2 * (chip ^ (1 << orders[core][stage])) + core)
        for chip in range(chips)
        for core in range(2)
    ]


def walker_rows(gathered, w):
    chips, _, part, basis = gathered.shape
    return gathered[:, w].reshape(chips * part, basis)


def tmat_half(lhs, green):
    vecs, m, basis = lhs.shape
    pack = max(1, ROWS // m)
    return jnp.concatenate(
        [
            lax.dot_general(
                lhs[g : g + pack].reshape(pack * m, basis), green, (((1,), (1,)), ((), ())),
                preferred_element_type=F32,
            ).astype(BF16)
            for g in range(0, vecs, pack)
        ],
        axis=0,
    )


def side_by_side(tmat, walkers, vecs):
    m, i = tmat.shape[0] // vecs, tmat.shape[1] // walkers
    return jnp.concatenate(
        [
            jnp.concatenate(
                [tmat[g * m : (g + 1) * m, w * i : (w + 1) * i] for g in range(vecs)], axis=1
            )
            for w in range(walkers)
        ],
        axis=0,
    )


def sweep(vecs, green, walkers, lhs_rows, rhs_rows, held, add):
    def step(k, carry):
        block = pl.ds(k * BLOCK, BLOCK)
        tmat = tmat_half(vecs[block, lhs_rows[0] : lhs_rows[1], :], green)
        held[...] = side_by_side(tmat, walkers, BLOCK)
        rhs = vecs[block, rhs_rows[0] : rhs_rows[1], :].reshape(-1, vecs.shape[2])
        add(jnp.dot(held[...], rhs, preferred_element_type=F32))
        return carry

    lax.fori_loop(0, vecs.shape[0] // BLOCK, step, 0)


def arrange_kernel(tables, part, first, source, *refs):
    out, sems = refs[-2:]
    index = lax.axis_index("chol")
    chip, core = index // 2, index % 2
    copies = []
    for k in range(source.shape[0] // COPIED):
        for pos, (a, b) in enumerate(zip(*tables)):
            at = pl.multiple_of((chip ^ jnp.where(core == 0, a, b)) * part, part)
            copies.append(
                pltpu.make_async_copy(
                    source.at[pl.ds(k * COPIED, COPIED), pl.ds(at, part), :],
                    out.at[pl.ds(first + k * COPIED, COPIED), pl.ds(pos * part, part), :],
                    sems.at[k, pos],
                )
            )
    for copy in copies:
        copy.start()
    for copy in copies:
        copy.wait()


def stacked(parts, walkers):
    return jnp.concatenate(
        [walker_rows(part, w) for w in range(walkers) for part in parts], axis=0
    )


def dots(values, target, energy):
    for w, value in enumerate(values):
        product = value * walker_rows(target, w).astype(F32)
        energy[w] = jnp.full(energy.shape[1:], jnp.sum(product), F32)


def first_kernel(gathered, vecs, total, energy, held):
    half, walkers, part, _ = gathered.shape
    span = half * part
    total[...] = jnp.zeros_like(total)

    def add(new):
        total[...] += new.reshape(total.shape)

    green = stacked([gathered], walkers)
    sweep(vecs, green, walkers, (0, 2 * span), (0, span), held, add)
    dots([total[w, :span, :] for w in range(walkers)], gathered, energy)


def quarter_kernel(quarter, early, late, vecs, total, out, *refs):
    acc, held = refs[-2:]
    count, walkers, part, _ = early.shape
    size = count * part
    first = quarter * size
    for w in range(walkers):
        acc[w * size : (w + 1) * size, :] = total[w, first : first + size, :]

    def add(new):
        acc[...] += new

    green = stacked([early, late], walkers)
    sweep(vecs, green, walkers, (first, first + size), (2 * size, 4 * size), held, add)
    values = [acc[w * size : (w + 1) * size, :] for w in range(walkers)]
    for w, value in enumerate(values):
        for pos in range(count):
            out[pos, w] = value[pos * part : (pos + 1) * part].astype(out.dtype)
    if quarter >= 2:
        twice = [value + total[w, first : first + size, :] for w, value in enumerate(values)]
        dots(twice, early if quarter == 2 else late, refs[0])


def arrange(tables, part, source, vecs=None):
    count = source.shape[0]
    args = (source,) if vecs is None else (source, vecs)
    return pl.pallas_call(
        functools.partial(arrange_kernel, tables, part, 0 if vecs is None else count),
        out_shape=jax.ShapeDtypeStruct((2 * count,) + source.shape[1:], source.dtype),
        in_specs=[HBM, VMEM][: len(args)],
        out_specs=VMEM,
        input_output_aliases={} if vecs is None else {1: 0},
        scratch_shapes=[pltpu.SemaphoreType.DMA((count // COPIED, len(tables[0])))],
        compiler_params=pltpu.CompilerParams(vmem_limit_bytes=8 << 20),
        cost_estimate=pl.CostEstimate(
            flops=0, bytes_accessed=4 * source.size, transcendentals=0
        ),
        name="arrange",
    )(*args)


def first_half(gathered, vecs):
    half, walkers, part, basis = gathered.shape
    count, occupied = vecs.shape[:2]
    return pl.pallas_call(
        first_kernel,
        out_shape=(
            jax.ShapeDtypeStruct((walkers, occupied, basis), F32),
            jax.ShapeDtypeStruct((walkers, 8, 128), F32),
        ),
        in_specs=[VMEM] * 2,
        out_specs=(VMEM, VMEM),
        scratch_shapes=[pltpu.VMEM((walkers * occupied, BLOCK * half * part), BF16)],
        compiler_params=pltpu.CompilerParams(vmem_limit_bytes=20 << 20),
        cost_estimate=pl.CostEstimate(
            flops=2 * walkers * count * occupied * occupied * basis,
            bytes_accessed=2 * count * occupied * basis,
            transcendentals=0,
        ),
        name="first_half",
    )(gathered, vecs)


def quarter_of(quarter, early, late, vecs, total):
    size, walkers, part, basis = early.shape
    count, occupied = vecs.shape[:2]
    leaves = quarter >= 2
    shapes = [jax.ShapeDtypeStruct(early.shape, BF16 if leaves else F32)]
    if leaves:
        shapes.append(jax.ShapeDtypeStruct((walkers, 8, 128), F32))
    return pl.pallas_call(
        functools.partial(quarter_kernel, quarter),
        out_shape=tuple(shapes),
        in_specs=[VMEM] * 4,
        out_specs=(VMEM,) * len(shapes),
        scratch_shapes=[
            pltpu.VMEM((walkers * size * part, basis), F32),
            pltpu.VMEM((walkers * size * part, 2 * BLOCK * size * part), BF16),
        ],
        compiler_params=pltpu.CompilerParams(vmem_limit_bytes=20 << 20),
        cost_estimate=pl.CostEstimate(
            flops=walkers * count * occupied * occupied * basis // 2,
            bytes_accessed=2 * early.size,
            transcendentals=0,
        ),
    )(early, late, vecs, total)


def shift(x, pairs):
    return lax.ppermute(x, "chol", pairs)


def per_device(green, chol_vecs, cotangent):
    size = lax.axis_size("chol")
    chips = size // 2
    bits = chips.bit_length() - 1
    orders = orders_of(bits)
    tables = [relative_chips(order) for order in orders]
    walkers, share, basis = green.shape
    pair = walkers // 2
    count, occupied = chol_vecs.shape[:2]
    scale = 1.0 / (occupied * count * size)
    core = lax.axis_index("chol") % 2
    swap = [(d, d ^ 1) for d in range(size)]

    far = stage_pairs(orders, chips, 0)
    cross = [(source, target ^ 1) for source, target in far]

    def ordered(same, opposite, axis):
        return jnp.where(
            core == 0,
            jnp.concatenate([same, opposite], axis=axis),
            jnp.concatenate([opposite, same], axis=axis),
        )

    def split(x, axis):
        return (
            lax.dynamic_index_in_dim(x, core, axis=axis, keepdims=False),
            lax.dynamic_index_in_dim(x, 1 - core, axis=axis, keepdims=False),
        )

    mine, theirs = split(green.reshape(2, pair, share, basis), 0)
    far_same = shift(mine, far)
    far_cross = shift(theirs, cross)
    near_cross = shift(theirs, swap)
    other = shift(chol_vecs, swap)
    gathered = jnp.stack(
        [ordered(mine, near_cross, 1), ordered(far_same, far_cross, 1)]
    )

    def pairs(stage):
        return stage_pairs(orders, chips, stage)

    for stage in range(1, bits - 2):
        got = lax.ppermute(gathered, "chol", pairs(stage))
        gathered = jnp.concatenate([gathered, got], axis=0)
    got = shift(gathered, pairs(bits - 2))
    early = shift(gathered, pairs(bits - 1))
    late = shift(got, pairs(bits - 1))
    gathered = jnp.concatenate([gathered, got], axis=0)

    vecs = arrange(tables, 2 * share, chol_vecs)
    vecs = arrange(tables, 2 * share, other, vecs)
    total, energy = first_half(gathered, vecs)

    send, part = quarter_of(3, early, late, vecs, total)
    energy = energy + part
    arrived3 = shift(send, pairs(bits - 1))
    send, part = quarter_of(2, early, late, vecs, total)
    energy = energy + part
    arrived2 = shift(send, pairs(bits - 1))
    energy = energy + shift(energy, pairs(bits - 1))
    (keep,) = quarter_of(1, early, late, vecs, total)
    send = (keep + arrived3.astype(F32)).astype(BF16)
    arrived1 = shift(send, pairs(bits - 2))
    energy = energy + shift(energy, pairs(bits - 2))
    (keep,) = quarter_of(0, early, late, vecs, total)
    keep = keep + arrived2.astype(F32) + arrived1.astype(F32)

    for stage in range(bits - 3, -1, -1):
        half = keep.shape[0] // 2
        arrived = shift(keep[half:].astype(BF16), pairs(stage))
        energy = energy + shift(energy, pairs(stage))
        keep = keep[:half] + arrived.astype(F32)

    here, away = split(keep.reshape(pair, 2, share, basis), 1)
    back = shift(away, swap)
    sums = ordered(energy, shift(energy, swap), 0)[:, 0, 0]
    grads = ordered(here, back, 0)
    return (-0.5 * scale * sums, -scale * cotangent[:, None, None] * grads)


def solution(mesh):
    placed = (P("groups", "chol", None), P("chol", None, None), P("groups"))
    return jax.shard_map(
        per_device,
        mesh=mesh,
        in_specs=placed,
        out_specs=(P("groups"), P("groups", "chol", None)),
        check_vma=False,
    )
```

```python
import functools

import jax
import jax.numpy as jnp
from jax import lax
from jax.experimental import pallas as pl
from jax.experimental.pallas import tpu as pltpu
from jax.sharding import PartitionSpec as P


BLOCK = 8
COPIED = 4
ROWS = 256
BF16 = jnp.bfloat16
F32 = jnp.float32
VMEM = pl.BlockSpec(memory_space=pltpu.VMEM)
HBM = pl.BlockSpec(memory_space=pltpu.HBM)


def orders_of(bits):
    down = list(range(bits - 1, -1, -1))
    return (down, down[:-2] + down[:-3:-1])


def relative_chips(order):
    table = [0]
    for bit in order:
        table = table + [entry ^ (1 << bit) for entry in table]
    return table


def stage_pairs(orders, chips, stage):
    return [
        (2 * chip + core, 2 * (chip ^ (1 << orders[core][stage])) + core)
        for chip in range(chips)
        for core in range(2)
    ]


def walker_rows(gathered, w):
    chips, _, part, basis = gathered.shape
    return gathered[:, w].reshape(chips * part, basis)


def tmat_half(lhs, green):
    vecs, m, basis = lhs.shape
    pack = max(1, ROWS // m)
    return jnp.concatenate(
        [
            lax.dot_general(
                lhs[g : g + pack].reshape(pack * m, basis), green, (((1,), (1,)), ((), ())),
                preferred_element_type=F32,
            ).astype(BF16)
            for g in range(0, vecs, pack)
        ],
        axis=0,
    )


def side_by_side(tmat, walkers, vecs):
    m, i = tmat.shape[0] // vecs, tmat.shape[1] // walkers
    return jnp.concatenate(
        [
            jnp.concatenate(
                [tmat[g * m : (g + 1) * m, w * i : (w + 1) * i] for g in range(vecs)], axis=1
            )
            for w in range(walkers)
        ],
        axis=0,
    )


def sweep(vecs, green, walkers, lhs_rows, rhs_rows, held, add):
    def step(k, carry):
        block = pl.ds(k * BLOCK, BLOCK)
        tmat = tmat_half(vecs[block, lhs_rows[0] : lhs_rows[1], :], green)
        held[...] = side_by_side(tmat, walkers, BLOCK)
        rhs = vecs[block, rhs_rows[0] : rhs_rows[1], :].reshape(-1, vecs.shape[2])
        add(jnp.dot(held[...], rhs, preferred_element_type=F32))
        return carry

    lax.fori_loop(0, vecs.shape[0] // BLOCK, step, 0)


def arrange_kernel(tables, part, first, source, *refs):
    out, sems = refs[-2:]
    index = lax.axis_index("chol")
    chip, core = index // 2, index % 2
    copies = []
    for k in range(source.shape[0] // COPIED):
        for pos, (a, b) in enumerate(zip(*tables)):
            at = pl.multiple_of((chip ^ jnp.where(core == 0, a, b)) * part, part)
            copies.append(
                pltpu.make_async_copy(
                    source.at[pl.ds(k * COPIED, COPIED), pl.ds(at, part), :],
                    out.at[pl.ds(first + k * COPIED, COPIED), pl.ds(pos * part, part), :],
                    sems.at[k, pos],
                )
            )
    for copy in copies:
        copy.start()
    for copy in copies:
        copy.wait()


def stacked(parts, walkers):
    return jnp.concatenate(
        [walker_rows(part, w) for w in range(walkers) for part in parts], axis=0
    )


def dots(values, target, energy):
    for w, value in enumerate(values):
        product = value * walker_rows(target, w).astype(F32)
        energy[w] = jnp.full(energy.shape[1:], jnp.sum(product), F32)


def first_kernel(gathered, vecs, total, energy, held):
    half, walkers, part, _ = gathered.shape
    span = half * part
    total[...] = jnp.zeros_like(total)

    def add(new):
        total[...] += new.reshape(total.shape)

    green = stacked([gathered], walkers)
    sweep(vecs, green, walkers, (0, 2 * span), (0, span), held, add)
    dots([total[w, :span, :] for w in range(walkers)], gathered, energy)


def quarter_kernel(quarter, got, vecs, total, out, *refs):
    acc, held = refs[-2:]
    half, walkers, part, _ = got.shape
    count = half // 2
    size = count * part
    first = quarter * size
    for w in range(walkers):
        acc[w * size : (w + 1) * size, :] = total[w, first : first + size, :]

    def add(new):
        acc[...] += new

    green = stacked([got], walkers)
    sweep(vecs, green, walkers, (first, first + size), (2 * size, 4 * size), held, add)
    values = [acc[w * size : (w + 1) * size, :] for w in range(walkers)]
    for w, value in enumerate(values):
        for pos in range(count):
            out[pos, w] = value[pos * part : (pos + 1) * part].astype(out.dtype)
    if quarter >= 2:
        twice = [value + total[w, first : first + size, :] for w, value in enumerate(values)]
        dots(twice, got[(quarter - 2) * count : (quarter - 1) * count], refs[0])


def arrange(tables, part, source, vecs=None):
    count = source.shape[0]
    args = (source,) if vecs is None else (source, vecs)
    return pl.pallas_call(
        functools.partial(arrange_kernel, tables, part, 0 if vecs is None else count),
        out_shape=jax.ShapeDtypeStruct((2 * count,) + source.shape[1:], source.dtype),
        in_specs=[HBM, VMEM][: len(args)],
        out_specs=VMEM,
        input_output_aliases={} if vecs is None else {1: 0},
        scratch_shapes=[pltpu.SemaphoreType.DMA((count // COPIED, len(tables[0])))],
        compiler_params=pltpu.CompilerParams(vmem_limit_bytes=8 << 20),
        cost_estimate=pl.CostEstimate(
            flops=0, bytes_accessed=4 * source.size, transcendentals=0
        ),
        name="arrange",
    )(*args)


def first_half(gathered, vecs):
    half, walkers, part, basis = gathered.shape
    count, occupied = vecs.shape[:2]
    return pl.pallas_call(
        first_kernel,
        out_shape=(
            jax.ShapeDtypeStruct((walkers, occupied, basis), F32),
            jax.ShapeDtypeStruct((walkers, 8, 128), F32),
        ),
        in_specs=[VMEM] * 2,
        out_specs=(VMEM, VMEM),
        scratch_shapes=[pltpu.VMEM((walkers * occupied, BLOCK * half * part), BF16)],
        compiler_params=pltpu.CompilerParams(vmem_limit_bytes=20 << 20),
        cost_estimate=pl.CostEstimate(
            flops=2 * walkers * count * occupied * occupied * basis,
            bytes_accessed=2 * count * occupied * basis,
            transcendentals=0,
        ),
        name="first_half",
    )(gathered, vecs)


def quarter_of(quarter, got, vecs, total):
    half, walkers, part, basis = got.shape
    size = half // 2
    count, occupied = vecs.shape[:2]
    leaves = quarter >= 2
    shapes = [jax.ShapeDtypeStruct((size,) + got.shape[1:], BF16 if leaves else F32)]
    if leaves:
        shapes.append(jax.ShapeDtypeStruct((walkers, 8, 128), F32))
    return pl.pallas_call(
        functools.partial(quarter_kernel, quarter),
        out_shape=tuple(shapes),
        in_specs=[VMEM] * 3,
        out_specs=(VMEM,) * len(shapes),
        scratch_shapes=[
            pltpu.VMEM((walkers * size * part, basis), F32),
            pltpu.VMEM((walkers * size * part, 2 * BLOCK * size * part), BF16),
        ],
        compiler_params=pltpu.CompilerParams(vmem_limit_bytes=20 << 20),
        cost_estimate=pl.CostEstimate(
            flops=walkers * count * occupied * occupied * basis // 2,
            bytes_accessed=2 * got.size,
            transcendentals=0,
        ),
    )(got, vecs, total)


def shift(x, pairs):
    return lax.ppermute(x, "chol", pairs)


def per_device(green, chol_vecs, cotangent):
    size = lax.axis_size("chol")
    chips = size // 2
    bits = chips.bit_length() - 1
    orders = orders_of(bits)
    tables = [relative_chips(order) for order in orders]
    walkers, share, basis = green.shape
    pair = walkers // 2
    count, occupied = chol_vecs.shape[:2]
    scale = 1.0 / (occupied * count * size)
    core = lax.axis_index("chol") % 2
    swap = [(d, d ^ 1) for d in range(size)]

    far = stage_pairs(orders, chips, 0)
    cross = [(source, target ^ 1) for source, target in far]

    def ordered(same, opposite, axis):
        return jnp.where(
            core == 0,
            jnp.concatenate([same, opposite], axis=axis),
            jnp.concatenate([opposite, same], axis=axis),
        )

    def split(x, axis):
        return (
            lax.dynamic_index_in_dim(x, core, axis=axis, keepdims=False),
            lax.dynamic_index_in_dim(x, 1 - core, axis=axis, keepdims=False),
        )

    mine, theirs = split(green.reshape(2, pair, share, basis), 0)
    far_same = shift(mine, far)
    far_cross = shift(theirs, cross)
    near_cross = shift(theirs, swap)
    other = shift(chol_vecs, swap)
    gathered = jnp.stack(
        [ordered(mine, near_cross, 1), ordered(far_same, far_cross, 1)]
    )

    def pairs(stage):
        return stage_pairs(orders, chips, stage)

    for stage in range(1, bits - 2):
        got = lax.ppermute(gathered, "chol", pairs(stage))
        gathered = jnp.concatenate([gathered, got], axis=0)
    got = shift(gathered, pairs(bits - 2))
    gathered = jnp.concatenate([gathered, got], axis=0)
    got = shift(gathered, pairs(bits - 1))

    vecs = arrange(tables, 2 * share, chol_vecs)
    vecs = arrange(tables, 2 * share, other, vecs)
    total, energy = first_half(gathered, vecs)

    send, part = quarter_of(3, got, vecs, total)
    energy = energy + part
    arrived3 = shift(send, pairs(bits - 1))
    send, part = quarter_of(2, got, vecs, total)
    energy = energy + part
    arrived2 = shift(send, pairs(bits - 1))
    energy = ordered(energy, shift(energy, swap), 0)
    (keep,) = quarter_of(1, got, vecs, total)
    send = (keep + arrived3.astype(F32)).astype(BF16)
    arrived1 = shift(send, pairs(bits - 2))
    energy = energy + shift(energy, pairs(bits - 1))
    (keep,) = quarter_of(0, got, vecs, total)
    energy = energy + shift(energy, pairs(bits - 2))
    keep = keep + arrived2.astype(F32) + arrived1.astype(F32)

    for stage in range(bits - 3, -1, -1):
        half = keep.shape[0] // 2
        arrived = shift(keep[half:].astype(BF16), pairs(stage))
        energy = energy + shift(energy, pairs(stage))
        keep = keep[:half] + arrived.astype(F32)

    here, away = split(keep.reshape(pair, 2, share, basis), 1)
    back = shift(away, swap)
    grads = ordered(here, back, 0)
    return (-0.5 * scale * energy[:, 0, 0], -scale * cotangent[:, None, None] * grads)


def solution(mesh):
    placed = (P("groups", "chol", None), P("chol", None, None), P("groups"))
    return jax.shard_map(
        per_device,
        mesh=mesh,
        in_specs=placed,
        out_specs=(P("groups"), P("groups", "chol", None)),
        check_vma=False,
    )
```
